512 devices in a mesh: space: 128 (over z, x, core), chan: 4 (over y).
Axes of the slice: x: 4, y: 4, z: 16, core: 2. Of those that a mesh axis runs over, the one named last changes fastest.
Arguments:
- features: bfloat16 [1024, 64, 512], P('space', 'chan'), may hold values from -6 to 6
- weight: bfloat16 [27, 64, 64], P(None, 'chan'), may hold values from -0.15625 to 0.15625
- cotangent: bfloat16 [1024, 64, 512], P('space', 'chan'), may hold values from -6 to 6
- neighbours: int32 [1024, 27], P('space'), may hold values from -1 to 1023, as said below
Outputs:
- output: bfloat16 [1024, 64, 512], P('space', 'chan')
- grad_input: bfloat16 [1024, 64, 512], P('space', 'chan')
- grad_weight: float32 [27, 64, 64], P(None, 'chan')
The draws below stay inside these ranges and needn't reach their ends.
Inputs may be any that keep to these rules, and one draw needn't show every extreme that they name: `neighbours`: row r lists, for the displacement (i, j, k) in the finite set (-1, 0, 1)^3 at entry 9 (i + 1) + 3 (j + 1) + (k + 1), the slot of the brick at that displacement in bricks, or -1 where the scene has none. Slot s belongs to device s // 8 of space, and a neighbour at first displacement i belongs to the device of index one's own + i. The relation is symmetric: if row r names s at entry m, row s names r at entry 26 - m. A device's occupied bricks fill its first slots, and the last device of space has all 8 slots occupied; an empty slot's row is all -1, no row names an empty slot, and an occupied brick's entry 13 is its own slot.
All inputs are finite; a program needn't handle non-finite values.
Results may differ from the reference program's by a relative error of at most 0.001.
Values may be sent and summed in bfloat16 or wider, within the bound.
A program may use at most 128 MiB of HBM per device.

```python
import jax
import jax.numpy as jnp
from jax import lax

CHANNELS = 64
B_DEV = 8
CROSS = 8
SLOTS = 1024
VOXELS = 524288
N_SPACE = 128


def draw_neighbours(key, part):
    cells = CROSS * CROSS
    key_count, key_full, key_perm = jax.random.split(jax.random.fold_in(key, 11), 3)
    devices = jnp.arange(N_SPACE, dtype=jnp.int32)
    loads = jax.random.randint(key_count, (N_SPACE,), B_DEV // 2, B_DEV + 1)
    busiest = jax.random.randint(key_full, (), 0, N_SPACE)
    loads = jnp.where((devices == busiest) | (devices == N_SPACE - 1), B_DEV, loads)
    orders = jax.vmap(lambda subkey: jax.random.permutation(subkey, cells))(jax.random.split(key_perm, N_SPACE))
    places = jnp.arange(B_DEV, dtype=jnp.int32)
    occupied = places[None, :] < loads[:, None]
    picked = jnp.sort(jnp.where(occupied, orders[:, :B_DEV], cells), axis=1).astype(jnp.int32)
    slot_ids = (devices[:, None] * B_DEV + places[None, :]).astype(jnp.int32)
    device_grid = jnp.broadcast_to(devices[:, None], picked.shape)
    lookup = jnp.full((N_SPACE, cells + 1), -1, jnp.int32)
    lookup = lookup.at[device_grid, picked].set(jnp.where(occupied, slot_ids, -1).astype(jnp.int32))
    lookup = lookup[:, :cells]
    row_y = picked // CROSS
    row_z = picked % CROSS
    entries = []
    for step_x in range(3):
        for step_y in range(3):
            for step_z in range(3):
                near_s = device_grid + step_x - 1
                near_y = row_y + step_y - 1
                near_z = row_z + step_z - 1
                inside = occupied & (near_s >= 0) & (near_s < N_SPACE) & (near_y >= 0) & (near_y < CROSS) & (near_z >= 0) & (near_z < CROSS)
                found = lookup[jnp.clip(near_s, 0, N_SPACE - 1), jnp.clip(near_y, 0, CROSS - 1) * CROSS + jnp.clip(near_z, 0, CROSS - 1)]
                entries.append(jnp.where(inside, found, -1))
    return jnp.stack(entries, axis=-1).reshape(N_SPACE * B_DEV, 27).astype(jnp.int32)


def steps_of(key, dims, cuts, least, largest):
    factor_of = 1.0
    for position, shards_of in cuts:
        draws = jax.random.uniform(jax.random.fold_in(jax.random.fold_in(key, 6), position), (shards_of,), jnp.float32, least / len(cuts), largest / len(cuts))
        factor_of = factor_of * jnp.repeat(jnp.exp(draws), dims[position] // shards_of).reshape((-1,) + (1,) * (len(dims) - 1 - position))
    return factor_of


def normal_values(rng, extent, deviation, most, shards=(), kind=jnp.bfloat16):
    values = jax.random.normal(rng, extent, jnp.float32) * deviation
    if len(shards) > 0:
        values = steps_of(rng, extent, shards, -0.22, 0.18) * values
    return jnp.clip(values, min=-most, max=most).astype(kind)


def setup_inputs(seed: int = 0) -> dict:
    splits = jax.random.split(jax.random.key(seed), 5)
    features = normal_values(splits[0], (SLOTS, CHANNELS, 512), 1.0, 6.0, ((0, 128), (1, 4)))
    weight = normal_values(splits[1], (27, CHANNELS, CHANNELS), (27 * CHANNELS) ** -0.5, 0.15625, ((1, 4),))
    cotangent = normal_values(splits[2], (SLOTS, CHANNELS, 512), 1.0, 6.0, ((0, 128), (1, 4)))
    neighbours = draw_neighbours(jax.random.fold_in(splits[4], 71), 0)
    return {"features": features, "weight": weight, "cotangent": cotangent, "neighbours": neighbours}


def assemble(source, table):
    spans = (slice(7, 8), slice(0, 8), slice(0, 1))
    layers = []
    for step_x in range(3):
        slabs = []
        for step_y in range(3):
            pieces = []
            for step_z in range(3):
                picked = jnp.take(source, table[:, 9 * step_x + 3 * step_y + step_z], axis=0)
                pieces.append(picked[:, :, spans[step_x], spans[step_y], spans[step_z]])
            slabs.append(jnp.concatenate(pieces, axis=4))
        layers.append(jnp.concatenate(slabs, axis=3))
    return jnp.concatenate(layers, axis=2)

def convolve(padded, kernel):
    running = jnp.zeros((padded.shape[0], kernel.shape[1], 8, 8, 8), padded.dtype)
    for step_x in range(3):
        for step_y in range(3):
            for step_z in range(3):
                window = padded[:, :, step_x:step_x + 8, step_y:step_y + 8, step_z:step_z + 8]
                running = running + jnp.einsum('oc,rcxyz->roxyz', kernel[9 * step_x + 3 * step_y + step_z], window)
    return running

def reference(features, weight, cotangent, neighbours):
    slot_total = features.shape[0]
    feat_full = features.astype(jnp.float32).reshape(slot_total, CHANNELS, 8, 8, 8)
    kernel_full = weight.astype(jnp.float32)
    table = jnp.where(neighbours < 0, slot_total, neighbours).astype(jnp.int32)
    blocks = table.reshape(-1, 8 * B_DEV, 27)

    def forward(feat, kernel):
        source = jnp.concatenate([feat, jnp.zeros((1, CHANNELS, 8, 8, 8), feat.dtype)], axis=0)

        def one_block(block_rows):
            return convolve(assemble(source, block_rows), kernel)
        result = lax.map(jax.checkpoint(one_block), blocks)
        return result.reshape(slot_total, CHANNELS, 8, 8, 8)
    output, pullback = jax.vjp(forward, feat_full, kernel_full)
    grad_feat, grad_kernel = pullback(cotangent.astype(jnp.float32).reshape(slot_total, CHANNELS, 8, 8, 8))
    return (output.reshape(slot_total, CHANNELS, 512).astype(jnp.bfloat16), grad_feat.reshape(slot_total, CHANNELS, 512).astype(jnp.bfloat16), grad_kernel * VOXELS ** (-0.5))
```

```python
import functools

import jax
import jax.numpy as jnp
from jax import lax
from jax.experimental import pallas as pl
from jax.experimental.pallas import tpu as pltpu
from jax.sharding import PartitionSpec as P

MESH = pl.DeviceIdType.MESH
BRICKS = 8
HALF = 4
SHARE = 16
KERNEL_TILES = 32


def push(source, target, send_sem, recv_sem, device):
    return pltpu.make_async_remote_copy(
        src_ref=source,
        dst_ref=target,
        send_sem=send_sem,
        recv_sem=recv_sem,
        device_id=device,
        device_id_type=MESH,
    )


def gather_kernel(
    n_space, feat, cot, planes, wcut, all_feat, all_cot, all_planes, all_wcut,
    local_sem, ring_send, ring_recv, fwd_send, fwd_recv, plane_send, plane_recv, w_send, w_recv,
):
    me = lax.axis_index("chan")
    here = lax.axis_index("space")
    right, left, across = lax.rem(me + 1, 4), lax.rem(me + 3, 4), lax.rem(me + 2, 4)
    after, before = lax.rem(here + 1, n_space), lax.rem(here + n_space - 1, n_space)

    barrier = pltpu.get_barrier_semaphore()
    for other in (right, left, across):
        pl.semaphore_signal(barrier, inc=1, device_id=(here, other), device_id_type=MESH)
    for place in (after, before):
        for turn in range(4):
            pl.semaphore_signal(
                barrier, inc=1, device_id=(place, lax.rem(me + turn, 4)), device_id_type=MESH
            )
    pl.semaphore_wait(barrier, 11)

    pairs = ((feat, all_feat), (cot, all_cot))
    firsts = []
    for order in range(2):
        for tensor, (own, every) in enumerate(pairs):
            for side, peer in enumerate((right, left)):
                half = order if side == 0 else 1 - order
                rows = pl.ds(HALF * half, HALF)
                copy = push(
                    own.at[rows], every.at[me, rows],
                    ring_send.at[side, half, tensor], ring_recv.at[side, half, tensor], (here, peer),
                )
                copy.start()
                firsts.append(copy)
    others = []
    for direction, place in enumerate((after, before)):
        for turn in range(4):
            copy = push(
                planes.at[direction], all_planes.at[direction, me],
                plane_send.at[direction, turn], plane_recv.at[direction, turn],
                (place, lax.rem(me + turn, 4)),
            )
            copy.start()
            others.append((copy, direction, turn))
    weights = []
    for turn in range(1, 4):
        peer = lax.rem(me + turn, 4)
        copy = push(
            wcut.at[peer], all_wcut.at[me], w_send.at[turn - 1], w_recv.at[turn - 1], (here, peer)
        )
        copy.start()
        weights.append((copy, turn))
    locals_ = [
        pltpu.make_async_copy(feat, all_feat.at[me], local_sem.at[0]),
        pltpu.make_async_copy(cot, all_cot.at[me], local_sem.at[1]),
        pltpu.make_async_copy(wcut.at[me], all_wcut.at[me], local_sem.at[2]),
    ]
    for copy in locals_:
        copy.start()

    seconds = []
    for tensor, (own, every) in enumerate(pairs):
        for side, (source, peer) in enumerate(((left, right), (right, left))):
            half = side
            rows = pl.ds(HALF * half, HALF)
            push(
                own.at[rows], every.at[source, rows],
                ring_send.at[side, half, tensor], ring_recv.at[side, half, tensor], (here, peer),
            ).wait_recv()
            copy = push(
                every.at[source, rows], every.at[source, rows],
                fwd_send.at[side, tensor], fwd_recv.at[side, tensor], (here, peer),
            )
            copy.start()
            seconds.append(copy)
    for tensor, (own, every) in enumerate(pairs):
        for side, source in enumerate((left, right)):
            half = 1 - side
            rows = pl.ds(HALF * half, HALF)
            push(
                own.at[rows], every.at[source, rows],
                ring_send.at[side, half, tensor], ring_recv.at[side, half, tensor], (here, source),
            ).wait_recv()
            rows = pl.ds(HALF * side, HALF)
            push(
                every.at[across, rows], every.at[across, rows],
                fwd_send.at[side, tensor], fwd_recv.at[side, tensor], (here, source),
            ).wait_recv()
    for copy, direction, turn in others:
        source = lax.rem(me + 4 - turn, 4)
        push(
            planes.at[direction], all_planes.at[direction, source],
            plane_send.at[direction, turn], plane_recv.at[direction, turn], (before, source),
        ).wait_recv()
    for copy, turn in weights:
        source = lax.rem(me + 4 - turn, 4)
        push(
            wcut.at[source], all_wcut.at[source], w_send.at[turn - 1], w_recv.at[turn - 1], (here, source)
        ).wait_recv()
    for copy in locals_:
        copy.wait()
    for copy in firsts + seconds:
        copy.wait_send()
    for copy, direction, turn in others:
        copy.wait_send()
    for copy, turn in weights:
        copy.wait_send()


def conv_kernel(
    scale, table, all_feat, all_cot, all_planes, cot, weight, wback,
    out, grad_in, grad_w, bricks, prev, nxt, wt, stage, rows, acc,
):
    zero = jnp.zeros((8, 8, 128), jnp.float32)
    for u in range(8):
        bricks[BRICKS, u] = zero
    prev[BRICKS] = zero
    nxt[BRICKS] = zero
    wt[96:128, :] = jnp.zeros((32, 1152), jnp.bfloat16)
    for a in range(3):
        for j in range(9):
            k = 9 * a + j
            wt[32 * a : 32 * a + 16, 128 * j : 128 * j + 128] = weight[k]
            wt[32 * a + 16 : 32 * a + 32, 128 * j : 128 * j + 128] = wback[26 - k]

    def turn_brick(s, carry):
        both = jnp.concatenate(
            [all_feat[:, s].reshape(64, 512), all_cot[:, s].reshape(64, 512)], axis=0
        )
        bricks[s] = both.astype(jnp.float32).T.reshape(8, 8, 8, 128)
        return carry

    lax.fori_loop(0, BRICKS, turn_brick, 0)
    for direction, held in enumerate((prev, nxt)):
        for pair in range(BRICKS // 2):
            both = jnp.concatenate(
                [all_planes[direction, :, t, pair].reshape(64, 128) for t in range(2)], axis=0
            )
            held[2 * pair : 2 * pair + 2] = both.astype(jnp.float32).T.reshape(2, 8, 8, 128)

    acc[...] = jnp.zeros(acc.shape, jnp.float32)

    def one_brick(r, carry):
        def slot(i, j, k):
            named = table[r, 9 * i + 3 * j + k]
            return jnp.where(named < 0, BRICKS, jnp.bitwise_and(named, BRICKS - 1))

        for i in range(3):
            for j in range(3):
                vs = (slice(7, 8), slice(0, 8), slice(0, 1))[j]
                ys = (slice(0, 1), slice(1, 9), slice(9, 10))[j]
                ids = [slot(i, j, k) for k in range(3)]
                for u in range(8) if i == 1 else (0,):
                    x = (0, u + 1, 9)[i]
                    if i == 1:
                        low, mid, high = [bricks[s, u, vs] for s in ids]
                    else:
                        low, mid, high = [(prev, None, nxt)[i][s, vs] for s in ids]
                    w = lax.broadcasted_iota(jnp.int32, mid.shape, 1)
                    stage[0, x, ys] = pltpu.roll(jnp.where(w == 7, low, mid), 1, 1)
                    stage[1, x, ys] = mid
                    stage[2, x, ys] = pltpu.roll(jnp.where(w == 0, high, mid), 7, 1)
        for b in range(3):
            for c in range(3):
                j = 3 * b + c
                for x in range(10):
                    rows[64 * x : 64 * x + 64, 128 * j : 128 * j + 128] = (
                        stage[c, x, b : b + 8].reshape(64, 128).astype(jnp.bfloat16)
                    )
        terms = lax.dot_general(
            rows[...], wt[...], (((1,), (1,)), ((), ())), preferred_element_type=jnp.float32
        )
        turned = terms.T
        total = (
            turned[0:32, 0:512]
            + pltpu.roll(turned[32:64], 640 - 64, 1)[:, 0:512]
            + turned[64:96, 128:640]
        )
        out[r] = total[0:16].astype(jnp.bfloat16)
        grad_in[r] = total[16:32].astype(jnp.bfloat16)
        wide = jnp.concatenate(
            [cot[r].astype(jnp.float32), jnp.zeros((SHARE, 128), jnp.float32)], axis=1
        )
        lifted = jnp.concatenate([wide, pltpu.roll(wide, 64, 1), pltpu.roll(wide, 128, 1)], axis=0)
        acc[...] += jnp.dot(
            lifted.astype(jnp.bfloat16), rows[...], preferred_element_type=jnp.float32
        )
        return carry

    lax.fori_loop(0, BRICKS, one_brick, 0)
    lane = lax.broadcasted_iota(jnp.int32, (8, 128), 1)
    for a in range(3):
        for j in range(9):
            term = acc[16 * a : 16 * a + 16, 128 * j : 128 * j + 128] * scale
            grad_w[9 * a + j] = jnp.where(lane < 64, term[0:8], pltpu.roll(term[8:16], 64, 1))
    for k in range(27, KERNEL_TILES):
        grad_w[k] = jnp.zeros((8, 128), jnp.float32)


def sum_kernel(
    inner, outer, part, result, pieces, tile, blocks, whole,
    a_send, a_recv, b_send, b_recv, c_send, c_recv, local_sem,
):
    here = lax.axis_index("space")
    chan = lax.axis_index("chan")
    rank = lax.rem(here, inner)
    block = here // inner
    share = KERNEL_TILES // inner

    barrier = pltpu.get_barrier_semaphore()

    def greet(d, carry):
        peer = block * inner + lax.rem(rank + d, inner)
        pl.semaphore_signal(barrier, inc=1, device_id=(peer, chan), device_id_type=MESH)
        return carry

    lax.fori_loop(1, inner, greet, 0)
    for d in range(1, outer):
        peer = lax.rem(block + d, outer) * inner + rank
        pl.semaphore_signal(barrier, inc=1, device_id=(peer, chan), device_id_type=MESH)
    pl.semaphore_wait(barrier, inner - 1 + outer - 1)

    def scatter(d):
        to = lax.rem(rank + d, inner)
        return push(
            part.at[pl.ds(to * share, share)], pieces.at[d], a_send.at[d], a_recv.at[d],
            (block * inner + to, chan),
        )

    def start_scatter(d, carry):
        scatter(d).start()
        return carry

    def wait_scatter(d, carry):
        scatter(d).wait()
        return carry

    lax.fori_loop(1, inner, start_scatter, 0)
    pieces[0] = part[pl.ds(rank * share, share)]
    lax.fori_loop(1, inner, wait_scatter, 0)
    tile[...] = jnp.sum(pieces[...], axis=0)

    exchanges = []
    for d in range(1, outer):
        peer = lax.rem(block + d, outer)
        copy = push(
            tile, blocks.at[block], b_send.at[d - 1], b_recv.at[d - 1], (peer * inner + rank, chan)
        )
        copy.start()
        exchanges.append(copy)
    own = pltpu.make_async_copy(tile, blocks.at[block], local_sem)
    own.start()
    own.wait()
    for copy in exchanges:
        copy.wait()
    mine = pl.ds(rank * share, share)
    whole[mine] = jnp.sum(blocks[...], axis=0)

    def spread(d):
        to = lax.rem(rank + d, inner)
        return push(
            whole.at[mine], whole.at[mine], c_send.at[d], c_recv.at[d], (block * inner + to, chan)
        )

    def start_spread(d, carry):
        spread(d).start()
        return carry

    def wait_spread(d, carry):
        origin = lax.rem(rank + inner - d, inner)
        theirs = pl.ds(origin * share, share)
        push(
            whole.at[theirs], whole.at[theirs], c_send.at[d], c_recv.at[d], (block * inner + origin, chan)
        ).wait_recv()
        return carry

    def sent_spread(d, carry):
        spread(d).wait_send()
        return carry

    lax.fori_loop(1, inner, start_spread, 0)
    lax.fori_loop(1, inner, wait_spread, 0)
    lax.fori_loop(1, inner, sent_spread, 0)
    for k in range(27):
        term = whole[k]
        result[k, 0:8] = term[:, 0:64]
        result[k, 8:16] = pltpu.roll(term, 64, 1)[:, 0:64]


def body(n_space, features, weight, cotangent, neighbours):
    inner = 32 if n_space % 32 == 0 else n_space // 2
    outer = n_space // inner
    vmem = pl.BlockSpec(memory_space=pltpu.VMEM)
    anyspace = pl.BlockSpec(memory_space=pl.ANY)
    smem = pl.BlockSpec(memory_space=pltpu.SMEM)
    bf16, f32 = jnp.bfloat16, jnp.float32

    sides = []
    for lanes in (slice(448, 512), slice(0, 64)):
        both = [
            jnp.concatenate([t[0::2, :, lanes], t[1::2, :, lanes]], axis=2) for t in (features, cotangent)
        ]
        sides.append(jnp.stack(both))
    planes = jnp.stack(sides)
    wcut = weight.transpose(2, 0, 1).reshape(4, SHARE, 27 * SHARE)

    dma = pltpu.SemaphoreType.DMA
    all_feat, all_cot, all_planes, all_wcut = pl.pallas_call(
        functools.partial(gather_kernel, n_space),
        out_shape=(
            jax.ShapeDtypeStruct((4, BRICKS, SHARE, 512), bf16),
            jax.ShapeDtypeStruct((4, BRICKS, SHARE, 512), bf16),
            jax.ShapeDtypeStruct((2, 4, 2, BRICKS // 2, SHARE, 128), bf16),
            jax.ShapeDtypeStruct((4, SHARE, 27 * SHARE), bf16),
        ),
        in_specs=[anyspace] * 4,
        out_specs=(vmem,) * 4,
        scratch_shapes=[
            dma((3,)), dma((2, 2, 2)), dma((2, 2, 2)), dma((2, 2)), dma((2, 2)),
            dma((2, 4)), dma((2, 4)), dma((3,)), dma((3,)),
        ],
        compiler_params=pltpu.CompilerParams(collective_id=0, has_side_effects=True),
        name="gather",
    )(features, cotangent, planes, wcut)

    wback = all_wcut.reshape(4, SHARE, 27, SHARE).transpose(2, 1, 0, 3).reshape(27, SHARE, 64)
    wback = jnp.pad(wback, ((0, 0), (0, 0), (64, 0)))
    wfore = jnp.pad(weight, ((0, 0), (0, 0), (0, 64)))

    voxels = n_space * BRICKS * 512
    output, grad_input, part = pl.pallas_call(
        functools.partial(conv_kernel, voxels ** (-0.5)),
        out_shape=(
            jax.ShapeDtypeStruct((BRICKS, SHARE, 512), bf16),
            jax.ShapeDtypeStruct((BRICKS, SHARE, 512), bf16),
            jax.ShapeDtypeStruct((KERNEL_TILES, 8, 128), f32),
        ),
        in_specs=[smem] + [vmem] * 6,
        out_specs=(vmem,) * 3,
        scratch_shapes=[
            pltpu.VMEM((BRICKS + 1, 8, 8, 8, 128), f32),
            pltpu.VMEM((BRICKS + 1, 8, 8, 128), f32),
            pltpu.VMEM((BRICKS + 1, 8, 8, 128), f32),
            pltpu.VMEM((128, 1152), bf16),
            pltpu.VMEM((3, 10, 10, 8, 128), f32),
            pltpu.VMEM((640, 1152), bf16),
            pltpu.VMEM((48, 1152), f32),
        ],
        compiler_params=pltpu.CompilerParams(vmem_limit_bytes=48 * 2**20),
        name="conv",
    )(neighbours, all_feat, all_cot, all_planes, cotangent, wfore, wback)

    share = KERNEL_TILES // inner
    grad_weight = pl.pallas_call(
        functools.partial(sum_kernel, inner, outer),
        out_shape=jax.ShapeDtypeStruct((27, SHARE, 64), f32),
        in_specs=[vmem],
        out_specs=vmem,
        scratch_shapes=[
            pltpu.VMEM((inner, share, 8, 128), f32),
            pltpu.VMEM((share, 8, 128), f32),
            pltpu.VMEM((outer, share, 8, 128), f32),
            pltpu.VMEM((KERNEL_TILES, 8, 128), f32),
            dma((inner,)), dma((inner,)), dma((outer - 1,)), dma((outer - 1,)),
            dma((inner,)), dma((inner,)), dma(()),
        ],
        compiler_params=pltpu.CompilerParams(collective_id=1, has_side_effects=True),
        name="sum",
    )(part)
    return (output, grad_input, grad_weight)


def solution(mesh):
    in_specs = (
        P("space", "chan", None),
        P(None, "chan", None),
        P("space", "chan", None),
        P("space", None),
    )
    out_specs = (P("space", "chan", None), P("space", "chan", None), P(None, "chan", None))
    return jax.shard_map(
        functools.partial(body, mesh.shape["space"]),
        mesh=mesh, in_specs=in_specs, out_specs=out_specs, check_vma=False,
    )
```

```python
import functools

import jax
import jax.numpy as jnp
from jax import lax
from jax.experimental import pallas as pl
from jax.experimental.pallas import tpu as pltpu
from jax.sharding import PartitionSpec as P

MESH = pl.DeviceIdType.MESH
BRICKS = 8
HALF = 4
SHARE = 16
KERNEL_TILES = 32


def push(source, target, send_sem, recv_sem, device):
    return pltpu.make_async_remote_copy(
        src_ref=source,
        dst_ref=target,
        send_sem=send_sem,
        recv_sem=recv_sem,
        device_id=device,
        device_id_type=MESH,
    )


def gather_kernel(
    n_space, feat, cot, planes, wcut, all_feat, all_cot, all_planes, all_wcut,
    local_sem, ring_send, ring_recv, fwd_send, fwd_recv, plane_send, plane_recv, w_send, w_recv,
):
    me = lax.axis_index("chan")
    here = lax.axis_index("space")
    right, left, across = lax.rem(me + 1, 4), lax.rem(me + 3, 4), lax.rem(me + 2, 4)
    after, before = lax.rem(here + 1, n_space), lax.rem(here + n_space - 1, n_space)

    barrier = pltpu.get_barrier_semaphore()
    for other in (right, left, across):
        pl.semaphore_signal(barrier, inc=1, device_id=(here, other), device_id_type=MESH)
    for place in (after, before):
        for turn in range(4):
            pl.semaphore_signal(
                barrier, inc=1, device_id=(place, lax.rem(me + turn, 4)), device_id_type=MESH
            )
    pl.semaphore_wait(barrier, 11)

    pairs = ((feat, all_feat), (cot, all_cot))
    firsts = []
    for order in range(2):
        for tensor, (own, every) in enumerate(pairs):
            for side, peer in enumerate((right, left)):
                half = order if side == 0 else 1 - order
                rows = pl.ds(HALF * half, HALF)
                copy = push(
                    own.at[rows], every.at[me, rows],
                    ring_send.at[side, half, tensor], ring_recv.at[side, half, tensor], (here, peer),
                )
                copy.start()
                firsts.append(copy)
    others = []
    for direction, place in enumerate((after, before)):
        for turn in range(4):
            copy = push(
                planes.at[direction], all_planes.at[direction, me],
                plane_send.at[direction, turn], plane_recv.at[direction, turn],
                (place, lax.rem(me + turn, 4)),
            )
            copy.start()
            others.append((copy, direction, turn))
    weights = []
    for turn in range(1, 4):
        peer = lax.rem(me + turn, 4)
        copy = push(
            wcut.at[peer], all_wcut.at[me], w_send.at[turn - 1], w_recv.at[turn - 1], (here, peer)
        )
        copy.start()
        weights.append((copy, turn))
    locals_ = [
        pltpu.make_async_copy(feat, all_feat.at[me], local_sem.at[0]),
        pltpu.make_async_copy(cot, all_cot.at[me], local_sem.at[1]),
        pltpu.make_async_copy(wcut.at[me], all_wcut.at[me], local_sem.at[2]),
    ]
    for copy in locals_:
        copy.start()

    seconds = []
    for tensor, (own, every) in enumerate(pairs):
        for side, (source, peer) in enumerate(((left, right), (right, left))):
            half = side
            rows = pl.ds(HALF * half, HALF)
            push(
                own.at[rows], every.at[source, rows],
                ring_send.at[side, half, tensor], ring_recv.at[side, half, tensor], (here, peer),
            ).wait_recv()
            copy = push(
                every.at[source, rows], every.at[source, rows],
                fwd_send.at[side, tensor], fwd_recv.at[side, tensor], (here, peer),
            )
            copy.start()
            seconds.append(copy)
    for tensor, (own, every) in enumerate(pairs):
        for side, source in enumerate((left, right)):
            half = 1 - side
            rows = pl.ds(HALF * half, HALF)
            push(
                own.at[rows], every.at[source, rows],
                ring_send.at[side, half, tensor], ring_recv.at[side, half, tensor], (here, source),
            ).wait_recv()
            rows = pl.ds(HALF * side, HALF)
            push(
                every.at[across, rows], every.at[across, rows],
                fwd_send.at[side, tensor], fwd_recv.at[side, tensor], (here, source),
            ).wait_recv()
    for copy, direction, turn in others:
        source = lax.rem(me + 4 - turn, 4)
        push(
            planes.at[direction], all_planes.at[direction, source],
            plane_send.at[direction, turn], plane_recv.at[direction, turn], (before, source),
        ).wait_recv()
    for copy, turn in weights:
        source = lax.rem(me + 4 - turn, 4)
        push(
            wcut.at[source], all_wcut.at[source], w_send.at[turn - 1], w_recv.at[turn - 1], (here, source)
        ).wait_recv()
    for copy in locals_:
        copy.wait()
    for copy in firsts + seconds:
        copy.wait_send()
    for copy, direction, turn in others:
        copy.wait_send()
    for copy, turn in weights:
        copy.wait_send()


def assemble_all(
    scale, table, all_feat, all_cot, all_planes, all_wcut, cot, weight, bricks, prev, nxt, wt, stage, rows, acc, part
):
    zero = jnp.zeros((8, 8, 128), jnp.float32)
    for u in range(8):
        bricks[BRICKS, u] = zero
    prev[BRICKS] = zero
    nxt[BRICKS] = zero
    wt[...] = jnp.zeros((128, 1152), jnp.bfloat16)
    lane = lax.broadcasted_iota(jnp.int32, (SHARE, 128), 1)
    for a in range(3):
        for j in range(9):
            k = 9 * a + j
            wt[32 * a : 32 * a + 16, 128 * j : 128 * j + 64] = weight[k]
            back = 26 - k
            block = jnp.zeros((SHARE, 128), jnp.float32)
            for p in range(4):
                start = 64 + SHARE * p
                piece = all_wcut[p, :, 128 * (back // 8) : 128 * (back // 8) + 128].astype(jnp.float32)
                piece = pltpu.roll(piece, (start - SHARE * (back % 8)) % 128, 1)
                block = jnp.where((lane >= start) & (lane < start + SHARE), piece, block)
            wt[32 * a + 16 : 32 * a + 32, 128 * j : 128 * j + 128] = block.astype(jnp.bfloat16)

    def turn_brick(s, carry):
        both = jnp.concatenate(
            [all_feat[:, s].reshape(64, 512), all_cot[:, s].reshape(64, 512)], axis=0
        )
        bricks[s] = both.astype(jnp.float32).T.reshape(8, 8, 8, 128)
        return carry

    lax.fori_loop(0, BRICKS, turn_brick, 0)
    for direction, held in enumerate((prev, nxt)):
        for pair in range(BRICKS // 2):
            both = jnp.concatenate(
                [all_planes[direction, :, t, pair].reshape(64, 128) for t in range(2)], axis=0
            )
            held[2 * pair : 2 * pair + 2] = both.astype(jnp.float32).T.reshape(2, 8, 8, 128)

    acc[...] = jnp.zeros(acc.shape, jnp.float32)

    def one_brick(r, carry):
        def slot(i, j, k):
            named = table[r, 9 * i + 3 * j + k]
            return jnp.where(named < 0, BRICKS, jnp.bitwise_and(named, BRICKS - 1))

        for i in range(3):
            for j in range(3):
                vs = (slice(7, 8), slice(0, 8), slice(0, 1))[j]
                ys = (slice(0, 1), slice(1, 9), slice(9, 10))[j]
                ids = [slot(i, j, k) for k in range(3)]
                for u in range(8) if i == 1 else (0,):
                    x = (0, u + 1, 9)[i]
                    if i == 1:
                        low, mid, high = [bricks[s, u, vs] for s in ids]
                    else:
                        low, mid, high = [(prev, None, nxt)[i][s, vs] for s in ids]
                    w = lax.broadcasted_iota(jnp.int32, mid.shape, 1)
                    stage[0, x, ys] = pltpu.roll(jnp.where(w == 7, low, mid), 1, 1)
                    stage[1, x, ys] = mid
                    stage[2, x, ys] = pltpu.roll(jnp.where(w == 0, high, mid), 7, 1)
        for b in range(3):
            for c in range(3):
                j = 3 * b + c
                for x in range(10):
                    rows[r, 64 * x : 64 * x + 64, 128 * j : 128 * j + 128] = (
                        stage[c, x, b : b + 8].reshape(64, 128).astype(jnp.bfloat16)
                    )
        wide = jnp.concatenate(
            [cot[r].astype(jnp.float32), jnp.zeros((SHARE, 128), jnp.float32)], axis=1
        )
        lifted = jnp.concatenate([wide, pltpu.roll(wide, 64, 1), pltpu.roll(wide, 128, 1)], axis=0)
        acc[...] += jnp.dot(
            lifted.astype(jnp.bfloat16), rows[r], preferred_element_type=jnp.float32
        )
        return carry

    lax.fori_loop(0, BRICKS, one_brick, 0)
    lane = lax.broadcasted_iota(jnp.int32, (8, 128), 1)
    for a in range(3):
        for j in range(9):
            term = acc[16 * a : 16 * a + 16, 128 * j : 128 * j + 128] * scale
            part[9 * a + j] = jnp.where(lane < 64, term[0:8], pltpu.roll(term[8:16], 64, 1))
    for k in range(27, KERNEL_TILES):
        part[k] = jnp.zeros((8, 128), jnp.float32)


def convolve(first, last, rows, wt, out, grad_in):
    def one_brick(r, carry):
        terms = lax.dot_general(
            rows[r], wt[...], (((1,), (1,)), ((), ())), preferred_element_type=jnp.float32
        )
        turned = terms.T
        total = (
            turned[0:32, 0:512]
            + pltpu.roll(turned[32:64], 640 - 64, 1)[:, 0:512]
            + turned[64:96, 128:640]
        )
        out[r] = total[0:16].astype(jnp.bfloat16)
        grad_in[r] = total[16:32].astype(jnp.bfloat16)
        return carry

    lax.fori_loop(first, last, one_brick, 0)


def conv_kernel(
    inner, outer, scale, table, all_feat, all_cot, all_planes, all_wcut, cot, weight,
    out, grad_in, result,
    bricks, prev, nxt, wt, stage, rows, acc, part, pieces, tile, blocks, whole,
    a_send, a_recv, b_send, b_recv, c_send, c_recv,
):
    here = lax.axis_index("space")
    chan = lax.axis_index("chan")
    rank = lax.rem(here, inner)
    block = here // inner
    share = KERNEL_TILES // inner

    barrier = pltpu.get_barrier_semaphore()

    def greet(d, carry):
        peer = block * inner + lax.rem(rank + d, inner)
        pl.semaphore_signal(barrier, inc=1, device_id=(peer, chan), device_id_type=MESH)
        return carry

    lax.fori_loop(1, inner, greet, 0)
    for d in range(1, outer):
        peer = lax.rem(block + d, outer) * inner + rank
        pl.semaphore_signal(barrier, inc=1, device_id=(peer, chan), device_id_type=MESH)
    assemble_all(
        scale, table, all_feat, all_cot, all_planes, all_wcut, cot, weight,
        bricks, prev, nxt, wt, stage, rows, acc, part,
    )
    pl.semaphore_wait(barrier, inner - 1 + outer - 1)

    def scatter(d):
        to = lax.rem(rank + d, inner)
        return push(
            part.at[pl.ds(to * share, share)], pieces.at[d], a_send.at[d], a_recv.at[d],
            (block * inner + to, chan),
        )

    def start_scatter(d, carry):
        scatter(d).start()
        return carry

    def wait_scatter(d, carry):
        scatter(d).wait()
        return carry

    lax.fori_loop(1, inner, start_scatter, 0)
    pieces[0] = part[pl.ds(rank * share, share)]
    convolve(0, BRICKS // 2, rows, wt, out, grad_in)
    lax.fori_loop(1, inner, wait_scatter, 0)
    tile[...] = jnp.sum(pieces[...], axis=0)

    exchanges = []
    for d in range(1, outer):
        peer = lax.rem(block + d, outer)
        copy = push(
            tile, blocks.at[block], b_send.at[d - 1], b_recv.at[d - 1], (peer * inner + rank, chan)
        )
        copy.start()
        exchanges.append(copy)
    blocks[block] = tile[...]
    convolve(BRICKS // 2, BRICKS, rows, wt, out, grad_in)
    for copy in exchanges:
        copy.wait()
    mine = pl.ds(rank * share, share)
    whole[mine] = jnp.sum(blocks[...], axis=0)

    def spread(d):
        to = lax.rem(rank + d, inner)
        return push(
            whole.at[mine], whole.at[mine], c_send.at[d], c_recv.at[d], (block * inner + to, chan)
        )

    def start_spread(d, carry):
        spread(d).start()
        return carry

    def wait_spread(d, carry):
        origin = lax.rem(rank + inner - d, inner)
        theirs = pl.ds(origin * share, share)
        push(
            whole.at[theirs], whole.at[theirs], c_send.at[d], c_recv.at[d], (block * inner + origin, chan)
        ).wait_recv()
        return carry

    def sent_spread(d, carry):
        spread(d).wait_send()
        return carry

    lax.fori_loop(1, inner, start_spread, 0)
    lax.fori_loop(1, inner, wait_spread, 0)
    lax.fori_loop(1, inner, sent_spread, 0)
    for k in range(27):
        term = whole[k]
        result[k, 0:8] = term[:, 0:64]
        result[k, 8:16] = pltpu.roll(term, 64, 1)[:, 0:64]


def body(n_space, features, weight, cotangent, neighbours):
    inner = 32 if n_space % 32 == 0 else n_space // 2
    outer = n_space // inner
    vmem = pl.BlockSpec(memory_space=pltpu.VMEM)
    anyspace = pl.BlockSpec(memory_space=pl.ANY)
    smem = pl.BlockSpec(memory_space=pltpu.SMEM)
    bf16, f32 = jnp.bfloat16, jnp.float32

    sides = []
    for lanes in (slice(448, 512), slice(0, 64)):
        both = [
            jnp.concatenate([t[0::2, :, lanes], t[1::2, :, lanes]], axis=2) for t in (features, cotangent)
        ]
        sides.append(jnp.stack(both))
    planes = jnp.stack(sides)
    wcut = weight.transpose(2, 0, 1).reshape(4, SHARE, 27 * SHARE)
    wcut = jnp.pad(wcut, ((0, 0), (0, 0), (0, 512 - 27 * SHARE)))

    dma = pltpu.SemaphoreType.DMA
    all_feat, all_cot, all_planes, all_wcut = pl.pallas_call(
        functools.partial(gather_kernel, n_space),
        out_shape=(
            jax.ShapeDtypeStruct((4, BRICKS, SHARE, 512), bf16),
            jax.ShapeDtypeStruct((4, BRICKS, SHARE, 512), bf16),
            jax.ShapeDtypeStruct((2, 4, 2, BRICKS // 2, SHARE, 128), bf16),
            jax.ShapeDtypeStruct((4, SHARE, 512), bf16),
        ),
        in_specs=[anyspace] * 4,
        out_specs=(vmem,) * 4,
        scratch_shapes=[
            dma((3,)), dma((2, 2, 2)), dma((2, 2, 2)), dma((2, 2)), dma((2, 2)),
            dma((2, 4)), dma((2, 4)), dma((3,)), dma((3,)),
        ],
        compiler_params=pltpu.CompilerParams(collective_id=0, has_side_effects=True),
        name="gather",
    )(features, cotangent, planes, wcut)

    voxels = n_space * BRICKS * 512
    share = KERNEL_TILES // inner
    output, grad_input, grad_weight = pl.pallas_call(
        functools.partial(conv_kernel, inner, outer, voxels ** (-0.5)),
        out_shape=(
            jax.ShapeDtypeStruct((BRICKS, SHARE, 512), bf16),
            jax.ShapeDtypeStruct((BRICKS, SHARE, 512), bf16),
            jax.ShapeDtypeStruct((27, SHARE, 64), f32),
        ),
        in_specs=[smem] + [vmem] * 6,
        out_specs=(vmem,) * 3,
        scratch_shapes=[
            pltpu.VMEM((BRICKS + 1, 8, 8, 8, 128), f32),
            pltpu.VMEM((BRICKS + 1, 8, 8, 128), f32),
            pltpu.VMEM((BRICKS + 1, 8, 8, 128), f32),
            pltpu.VMEM((128, 1152), bf16),
            pltpu.VMEM((3, 10, 10, 8, 128), f32),
            pltpu.VMEM((BRICKS, 640, 1152), bf16),
            pltpu.VMEM((48, 1152), f32),
            pltpu.VMEM((KERNEL_TILES, 8, 128), f32),
            pltpu.VMEM((inner, share, 8, 128), f32),
            pltpu.VMEM((share, 8, 128), f32),
            pltpu.VMEM((outer, share, 8, 128), f32),
            pltpu.VMEM((KERNEL_TILES, 8, 128), f32),
            dma((inner,)), dma((inner,)), dma((outer - 1,)), dma((outer - 1,)),
            dma((inner,)), dma((inner,)),
        ],
        compiler_params=pltpu.CompilerParams(
            collective_id=1, has_side_effects=True, vmem_limit_bytes=48 * 2**20
        ),
        name="conv",
    )(neighbours, all_feat, all_cot, all_planes, all_wcut, cotangent, weight)
    return (output, grad_input, grad_weight)


def solution(mesh):
    in_specs = (
        P("space", "chan", None),
        P(None, "chan", None),
        P("space", "chan", None),
        P("space", None),
    )
    out_specs = (P("space", "chan", None), P("space", "chan", None), P(None, "chan", None))
    return jax.shard_map(
        functools.partial(body, mesh.shape["space"]),
        mesh=mesh, in_specs=in_specs, out_specs=out_specs, check_vma=False,
    )
```

```python
import functools

import jax
import jax.numpy as jnp
from jax import lax
from jax.experimental import pallas as pl
from jax.experimental.pallas import tpu as pltpu
from jax.sharding import PartitionSpec as P

MESH = pl.DeviceIdType.MESH
BRICKS = 8
HALF = 4
SHARE = 16
KERNEL_TILES = 32


def push(source, target, send_sem, recv_sem, device):
    return pltpu.make_async_remote_copy(
        src_ref=source,
        dst_ref=target,
        send_sem=send_sem,
        recv_sem=recv_sem,
        device_id=device,
        device_id_type=MESH,
    )


def gather_kernel(
    n_space, feat, cot, planes, wcut, all_feat, all_cot, all_planes, all_wcut,
    ring_send, ring_recv, fwd_send, fwd_recv, face_send, face_recv,
    side_send, side_recv, last_send, last_recv, w_send, w_recv,
):
    me = lax.axis_index("chan")
    here = lax.axis_index("space")
    right, left, across = lax.rem(me + 1, 4), lax.rem(me + 3, 4), lax.rem(me + 2, 4)
    after, before = lax.rem(here + 1, n_space), lax.rem(here + n_space - 1, n_space)

    barrier = pltpu.get_barrier_semaphore()
    for other in (right, left, across):
        pl.semaphore_signal(barrier, inc=1, device_id=(here, other), device_id_type=MESH)
    for place in (after, before):
        pl.semaphore_signal(barrier, inc=1, device_id=(place, me), device_id_type=MESH)
    pl.semaphore_wait(barrier, 5)

    peers = (right, left)
    sources = (left, right)
    pairs = ((feat, all_feat), (cot, all_cot))

    def face(direction):
        return push(
            planes.at[direction], all_planes.at[direction, me],
            face_send.at[direction], face_recv.at[direction], ((after, before)[direction], me),
        )

    def ring(side, half, tensor, owner):
        own, every = pairs[tensor]
        rows = pl.ds(HALF * half, HALF)
        return push(
            own.at[rows], every.at[owner, rows],
            ring_send.at[side, half, tensor], ring_recv.at[side, half, tensor], (here, peers[side]),
        )

    def relay(side, tensor, owner):
        every = pairs[tensor][1]
        rows = pl.ds(HALF * side, HALF)
        return push(
            every.at[owner, rows], every.at[owner, rows],
            fwd_send.at[side, tensor], fwd_recv.at[side, tensor], (here, peers[side]),
        )

    def beside(side, direction, owner):
        return push(
            all_planes.at[direction, owner], all_planes.at[direction, owner],
            side_send.at[side, direction], side_recv.at[side, direction], (here, peers[side]),
        )

    def onward(side, owner):
        return push(
            all_planes.at[side, owner], all_planes.at[side, owner],
            last_send.at[side], last_recv.at[side], (here, peers[side]),
        )

    def columns(turn, owner, peer):
        return push(
            wcut.at[peer], all_wcut.at[owner], w_send.at[turn - 1], w_recv.at[turn - 1], (here, peer)
        )

    sent = []

    def go(copy):
        copy.start()
        sent.append(copy)

    for direction in range(2):
        go(face(direction))
    for tensor in range(2):
        for side in range(2):
            go(ring(side, side, tensor, me))
    for direction in range(2):
        face(direction).wait_recv()
    for direction in range(2):
        for side in range(2):
            go(beside(side, side ^ direction, me))
    for turn in range(1, 4):
        go(columns(turn, me, lax.rem(me + turn, 4)))
    for tensor in range(2):
        for side in range(2):
            go(ring(side, 1 - side, tensor, me))
    for tensor in range(2):
        for side in range(2):
            ring(side, side, tensor, sources[side]).wait_recv()
            go(relay(side, tensor, sources[side]))
    for side in range(2):
        beside(side, side, sources[side]).wait_recv()
        go(onward(side, sources[side]))
    for side in range(2):
        beside(side, 1 - side, sources[side]).wait_recv()
    for turn in range(1, 4):
        origin = lax.rem(me + 4 - turn, 4)
        columns(turn, origin, origin).wait_recv()
    for side in range(2):
        for tensor in range(2):
            ring(side, 1 - side, tensor, sources[side]).wait_recv()
            relay(side, tensor, across).wait_recv()
        onward(side, across).wait_recv()
    for copy in sent:
        copy.wait_send()


def assemble_all(
    scale, table, all_feat, all_cot, all_planes, all_wcut, cot, weight, bricks, prev, nxt, wt, stage, rows, acc, part
):
    zero = jnp.zeros((8, 8, 128), jnp.float32)
    for u in range(8):
        bricks[BRICKS, u] = zero
    prev[BRICKS] = zero
    nxt[BRICKS] = zero
    wt[...] = jnp.zeros((128, 1152), jnp.bfloat16)
    lane = lax.broadcasted_iota(jnp.int32, (SHARE, 128), 1)
    for a in range(3):
        for j in range(9):
            k = 9 * a + j
            wt[32 * a : 32 * a + 16, 128 * j : 128 * j + 64] = weight[k]
            back = 26 - k
            block = jnp.zeros((SHARE, 128), jnp.float32)
            for p in range(4):
                start = 64 + SHARE * p
                piece = all_wcut[p, :, 128 * (back // 8) : 128 * (back // 8) + 128].astype(jnp.float32)
                piece = pltpu.roll(piece, (start - SHARE * (back % 8)) % 128, 1)
                block = jnp.where((lane >= start) & (lane < start + SHARE), piece, block)
            wt[32 * a + 16 : 32 * a + 32, 128 * j : 128 * j + 128] = block.astype(jnp.bfloat16)

    def turn_brick(s, carry):
        both = jnp.concatenate(
            [all_feat[:, s].reshape(64, 512), all_cot[:, s].reshape(64, 512)], axis=0
        )
        bricks[s] = both.astype(jnp.float32).T.reshape(8, 8, 8, 128)
        return carry

    lax.fori_loop(0, BRICKS, turn_brick, 0)
    for direction, held in enumerate((prev, nxt)):
        for pair in range(BRICKS // 2):
            both = jnp.concatenate(
                [all_planes[direction, :, t, pair].reshape(64, 128) for t in range(2)], axis=0
            )
            held[2 * pair : 2 * pair + 2] = both.astype(jnp.float32).T.reshape(2, 8, 8, 128)

    acc[...] = jnp.zeros(acc.shape, jnp.float32)

    def one_brick(r, carry):
        def slot(i, j, k):
            named = table[r, 9 * i + 3 * j + k]
            return jnp.where(named < 0, BRICKS, jnp.bitwise_and(named, BRICKS - 1))

        for i in range(3):
            for j in range(3):
                vs = (slice(7, 8), slice(0, 8), slice(0, 1))[j]
                ys = (slice(0, 1), slice(1, 9), slice(9, 10))[j]
                ids = [slot(i, j, k) for k in range(3)]
                for u in range(8) if i == 1 else (0,):
                    x = (0, u + 1, 9)[i]
                    if i == 1:
                        low, mid, high = [bricks[s, u, vs] for s in ids]
                    else:
                        low, mid, high = [(prev, None, nxt)[i][s, vs] for s in ids]
                    w = lax.broadcasted_iota(jnp.int32, mid.shape, 1)
                    stage[0, x, ys] = pltpu.roll(jnp.where(w == 7, low, mid), 1, 1)
                    stage[1, x, ys] = mid
                    stage[2, x, ys] = pltpu.roll(jnp.where(w == 0, high, mid), 7, 1)
        for b in range(3):
            for c in range(3):
                j = 3 * b + c
                for x in range(10):
                    rows[r, 64 * x : 64 * x + 64, 128 * j : 128 * j + 128] = (
                        stage[c, x, b : b + 8].reshape(64, 128).astype(jnp.bfloat16)
                    )
        wide = jnp.concatenate(
            [cot[r].astype(jnp.float32), jnp.zeros((SHARE, 128), jnp.float32)], axis=1
        )
        lifted = jnp.concatenate([wide, pltpu.roll(wide, 64, 1), pltpu.roll(wide, 128, 1)], axis=0)
        acc[...] += jnp.dot(
            lifted.astype(jnp.bfloat16), rows[r], preferred_element_type=jnp.float32
        )
        return carry

    lax.fori_loop(0, BRICKS, one_brick, 0)
    lane = lax.broadcasted_iota(jnp.int32, (8, 128), 1)
    for a in range(3):
        for j in range(9):
            term = acc[16 * a : 16 * a + 16, 128 * j : 128 * j + 128] * scale
            part[9 * a + j] = jnp.where(lane < 64, term[0:8], pltpu.roll(term[8:16], 64, 1))
    for k in range(27, KERNEL_TILES):
        part[k] = jnp.zeros((8, 128), jnp.float32)


def convolve(first, last, rows, wt, out, grad_in):
    def one_brick(r, carry):
        terms = lax.dot_general(
            rows[r], wt[...], (((1,), (1,)), ((), ())), preferred_element_type=jnp.float32
        )
        turned = terms.T
        total = (
            turned[0:32, 0:512]
            + pltpu.roll(turned[32:64], 640 - 64, 1)[:, 0:512]
            + turned[64:96, 128:640]
        )
        out[r] = total[0:16].astype(jnp.bfloat16)
        grad_in[r] = total[16:32].astype(jnp.bfloat16)
        return carry

    lax.fori_loop(first, last, one_brick, 0)


def conv_kernel(
    inner, outer, scale, table_at, feat_at, cot_at, planes_at, wcut_at, own_feat, own_cot, own_wcut, cot, weight,
    out, grad_in, result, table, all_feat, all_cot, all_planes, all_wcut, load_sem,
    bricks, prev, nxt, wt, stage, rows, acc, part, pieces, tile, blocks, whole,
    a_send, a_recv, b_send, b_recv, c_send, c_recv,
):
    here = lax.axis_index("space")
    chan = lax.axis_index("chan")
    rank = lax.rem(here, inner)
    block = here // inner
    share = KERNEL_TILES // inner

    barrier = pltpu.get_barrier_semaphore()

    def greet(d, carry):
        peer = block * inner + lax.rem(rank + d, inner)
        pl.semaphore_signal(barrier, inc=1, device_id=(peer, chan), device_id_type=MESH)
        return carry

    lax.fori_loop(1, inner, greet, 0)
    for d in range(1, outer):
        peer = lax.rem(block + d, outer) * inner + rank
        pl.semaphore_signal(barrier, inc=1, device_id=(peer, chan), device_id_type=MESH)
    loads = [
        pltpu.make_async_copy(table_at, table, load_sem.at[0]),
        pltpu.make_async_copy(planes_at, all_planes, load_sem.at[1]),
        pltpu.make_async_copy(own_feat, all_feat.at[chan], load_sem.at[2]),
        pltpu.make_async_copy(own_cot, all_cot.at[chan], load_sem.at[3]),
        pltpu.make_async_copy(own_wcut.at[chan], all_wcut.at[chan], load_sem.at[4]),
    ]
    for turn in range(1, 4):
        origin = lax.rem(chan + turn, 4)
        for place, (source, target) in enumerate(
            ((feat_at, all_feat), (cot_at, all_cot), (wcut_at, all_wcut))
        ):
            loads.append(
                pltpu.make_async_copy(
                    source.at[origin], target.at[origin], load_sem.at[2 + 3 * turn + place]
                )
            )
    for copy in loads:
        copy.start()
    for copy in loads:
        copy.wait()
    assemble_all(
        scale, table, all_feat, all_cot, all_planes, all_wcut, cot, weight,
        bricks, prev, nxt, wt, stage, rows, acc, part,
    )
    pl.semaphore_wait(barrier, inner - 1 + outer - 1)

    def scatter(d):
        to = lax.rem(rank + d, inner)
        return push(
            part.at[pl.ds(to * share, share)], pieces.at[d], a_send.at[d], a_recv.at[d],
            (block * inner + to, chan),
        )

    def start_scatter(d, carry):
        scatter(d).start()
        return carry

    def wait_scatter(d, carry):
        scatter(d).wait()
        return carry

    lax.fori_loop(1, inner, start_scatter, 0)
    pieces[0] = part[pl.ds(rank * share, share)]
    convolve(0, BRICKS // 2, rows, wt, out, grad_in)
    lax.fori_loop(1, inner, wait_scatter, 0)
    tile[...] = jnp.sum(pieces[...], axis=0)

    exchanges = []
    for d in range(1, outer):
        peer = lax.rem(block + d, outer)
        copy = push(
            tile, blocks.at[block], b_send.at[d - 1], b_recv.at[d - 1], (peer * inner + rank, chan)
        )
        copy.start()
        exchanges.append(copy)
    blocks[block] = tile[...]
    convolve(BRICKS // 2, BRICKS, rows, wt, out, grad_in)
    for copy in exchanges:
        copy.wait()
    mine = pl.ds(rank * share, share)
    whole[mine] = jnp.sum(blocks[...], axis=0)

    def spread(d):
        to = lax.rem(rank + d, inner)
        return push(
            whole.at[mine], whole.at[mine], c_send.at[d], c_recv.at[d], (block * inner + to, chan)
        )

    def start_spread(d, carry):
        spread(d).start()
        return carry

    def wait_spread(d, carry):
        origin = lax.rem(rank + inner - d, inner)
        theirs = pl.ds(origin * share, share)
        push(
            whole.at[theirs], whole.at[theirs], c_send.at[d], c_recv.at[d], (block * inner + origin, chan)
        ).wait_recv()
        return carry

    def sent_spread(d, carry):
        spread(d).wait_send()
        return carry

    lax.fori_loop(1, inner, start_spread, 0)
    lax.fori_loop(1, inner, wait_spread, 0)
    lax.fori_loop(1, inner, sent_spread, 0)
    for k in range(27):
        term = whole[k]
        result[k, 0:8] = term[:, 0:64]
        result[k, 8:16] = pltpu.roll(term, 64, 1)[:, 0:64]


def body(n_space, features, weight, cotangent, neighbours):
    inner = 32 if n_space % 32 == 0 else n_space // 2
    outer = n_space // inner
    vmem = pl.BlockSpec(memory_space=pltpu.VMEM)
    anyspace = pl.BlockSpec(memory_space=pl.ANY)
    bf16, f32 = jnp.bfloat16, jnp.float32

    sides = []
    for lanes in (slice(448, 512), slice(0, 64)):
        both = [
            jnp.concatenate([t[0::2, :, lanes], t[1::2, :, lanes]], axis=2) for t in (features, cotangent)
        ]
        sides.append(jnp.stack(both))
    planes = jnp.stack(sides)
    wcut = weight.transpose(2, 0, 1).reshape(4, SHARE, 27 * SHARE)
    wcut = jnp.pad(wcut, ((0, 0), (0, 0), (0, 512 - 27 * SHARE)))

    dma = pltpu.SemaphoreType.DMA
    all_feat, all_cot, all_planes, all_wcut = pl.pallas_call(
        functools.partial(gather_kernel, n_space),
        out_shape=(
            jax.ShapeDtypeStruct((4, BRICKS, SHARE, 512), bf16),
            jax.ShapeDtypeStruct((4, BRICKS, SHARE, 512), bf16),
            jax.ShapeDtypeStruct((2, 4, 2, BRICKS // 2, SHARE, 128), bf16),
            jax.ShapeDtypeStruct((4, SHARE, 512), bf16),
        ),
        in_specs=[anyspace] * 4,
        out_specs=(anyspace,) * 4,
        scratch_shapes=[
            dma((2, 2, 2)), dma((2, 2, 2)), dma((2, 2)), dma((2, 2)), dma((2,)), dma((2,)),
            dma((2, 2)), dma((2, 2)), dma((2,)), dma((2,)), dma((3,)), dma((3,)),
        ],
        compiler_params=pltpu.CompilerParams(collective_id=0, has_side_effects=True),
        name="gather",
    )(features, cotangent, planes, wcut)

    voxels = n_space * BRICKS * 512
    share = KERNEL_TILES // inner
    output, grad_input, grad_weight = pl.pallas_call(
        functools.partial(conv_kernel, inner, outer, voxels ** (-0.5)),
        out_shape=(
            jax.ShapeDtypeStruct((BRICKS, SHARE, 512), bf16),
            jax.ShapeDtypeStruct((BRICKS, SHARE, 512), bf16),
            jax.ShapeDtypeStruct((27, SHARE, 64), f32),
        ),
        in_specs=[pl.BlockSpec(memory_space=pltpu.HBM)] * 8 + [vmem] * 2,
        out_specs=(vmem,) * 3,
        scratch_shapes=[
            pltpu.SMEM((BRICKS, 27), jnp.int32),
            pltpu.VMEM((4, BRICKS, SHARE, 512), bf16),
            pltpu.VMEM((4, BRICKS, SHARE, 512), bf16),
            pltpu.VMEM((2, 4, 2, BRICKS // 2, SHARE, 128), bf16),
            pltpu.VMEM((4, SHARE, 512), bf16),
            dma((14,)),
            pltpu.VMEM((BRICKS + 1, 8, 8, 8, 128), f32),
            pltpu.VMEM((BRICKS + 1, 8, 8, 128), f32),
            pltpu.VMEM((BRICKS + 1, 8, 8, 128), f32),
            pltpu.VMEM((128, 1152), bf16),
            pltpu.VMEM((3, 10, 10, 8, 128), f32),
            pltpu.VMEM((BRICKS, 640, 1152), bf16),
            pltpu.VMEM((48, 1152), f32),
            pltpu.VMEM((KERNEL_TILES, 8, 128), f32),
            pltpu.VMEM((inner, share, 8, 128), f32),
            pltpu.VMEM((share, 8, 128), f32),
            pltpu.VMEM((outer, share, 8, 128), f32),
            pltpu.VMEM((KERNEL_TILES, 8, 128), f32),
            dma((inner,)), dma((inner,)), dma((outer - 1,)), dma((outer - 1,)),
            dma((inner,)), dma((inner,)),
        ],
        compiler_params=pltpu.CompilerParams(
            collective_id=1, has_side_effects=True, vmem_limit_bytes=63 * 2**20
        ),
        name="conv",
    )(
        neighbours, all_feat, all_cot, all_planes, all_wcut, features, cotangent, wcut, cotangent, weight
    )
    return (output, grad_input, grad_weight)


def solution(mesh):
    in_specs = (
        P("space", "chan", None),
        P(None, "chan", None),
        P("space", "chan", None),
        P("space", None),
    )
    out_specs = (P("space", "chan", None), P("space", "chan", None), P(None, "chan", None))
    return jax.shard_map(
        functools.partial(body, mesh.shape["space"]),
        mesh=mesh, in_specs=in_specs, out_specs=out_specs, check_vma=False,
    )
```

```python
import functools

import jax
import jax.numpy as jnp
from jax import lax
from jax.experimental import pallas as pl
from jax.experimental.pallas import tpu as pltpu
from jax.sharding import PartitionSpec as P

MESH = pl.DeviceIdType.MESH
BRICKS = 8
HALF = 4
SHARE = 16
KERNEL_TILES = 32


def push(source, target, send_sem, recv_sem, device):
    return pltpu.make_async_remote_copy(
        src_ref=source,
        dst_ref=target,
        send_sem=send_sem,
        recv_sem=recv_sem,
        device_id=device,
        device_id_type=MESH,
    )


def pack(feat, cot, weight, planes, wcut):
    lane = lax.broadcasted_iota(jnp.int32, (SHARE, 128), 1)
    for t, tensor in enumerate((feat, cot)):
        for pair in range(BRICKS // 2):
            for direction, lanes in enumerate((slice(384, 512), slice(0, 128))):
                first = tensor[2 * pair, :, lanes].astype(jnp.float32)
                second = tensor[2 * pair + 1, :, lanes].astype(jnp.float32)
                if direction == 0:
                    first = pltpu.roll(first, 64, 1)
                else:
                    second = pltpu.roll(second, 64, 1)
                planes[direction, t, pair] = jnp.where(lane < 64, first, second).astype(jnp.bfloat16)
    for g in range(4):
        count = min(8, 27 - 8 * g)
        block = weight[8 * g : 8 * g + count].reshape(SHARE * count, 64).astype(jnp.float32)
        if count < 8:
            block = jnp.concatenate([block, jnp.zeros((128 - SHARE * count, 64), jnp.float32)], axis=0)
        wcut[:, :, 128 * g : 128 * g + 128] = block.T.reshape(4, SHARE, 128).astype(jnp.bfloat16)


def gather_kernel(
    n_space, feat, cot, weight, all_feat, all_cot, all_planes, all_wcut,
    feat_here, cot_here, weight_here, planes, wcut, local_sem,
    ring_send, ring_recv, fwd_send, fwd_recv, face_send, face_recv,
    side_send, side_recv, last_send, last_recv, w_send, w_recv,
):
    me = lax.axis_index("chan")
    here = lax.axis_index("space")
    right, left, across = lax.rem(me + 1, 4), lax.rem(me + 3, 4), lax.rem(me + 2, 4)
    after, before = lax.rem(here + 1, n_space), lax.rem(here + n_space - 1, n_space)

    loads = [
        pltpu.make_async_copy(source, target, local_sem.at[place])
        for place, (source, target) in enumerate(
            ((feat, feat_here), (cot, cot_here), (weight, weight_here))
        )
    ]
    for copy in loads:
        copy.start()
    barrier = pltpu.get_barrier_semaphore()
    for other in (right, left, across):
        pl.semaphore_signal(barrier, inc=1, device_id=(here, other), device_id_type=MESH)
    for place in (after, before):
        pl.semaphore_signal(barrier, inc=1, device_id=(place, me), device_id_type=MESH)
    for copy in loads:
        copy.wait()
    pack(feat_here, cot_here, weight_here, planes, wcut)
    kept = pltpu.make_async_copy(wcut.at[me], all_wcut.at[me], local_sem.at[3])
    kept.start()
    pl.semaphore_wait(barrier, 5)

    peers = (right, left)
    sources = (left, right)
    pairs = ((feat, all_feat), (cot, all_cot))

    def face(direction):
        return push(
            planes.at[direction], all_planes.at[direction, me],
            face_send.at[direction], face_recv.at[direction], ((after, before)[direction], me),
        )

    def ring(side, half, tensor, owner):
        own, every = pairs[tensor]
        rows = pl.ds(HALF * half, HALF)
        return push(
            own.at[rows], every.at[owner, rows],
            ring_send.at[side, half, tensor], ring_recv.at[side, half, tensor], (here, peers[side]),
        )

    def relay(side, tensor, owner):
        every = pairs[tensor][1]
        rows = pl.ds(HALF * side, HALF)
        return push(
            every.at[owner, rows], every.at[owner, rows],
            fwd_send.at[side, tensor], fwd_recv.at[side, tensor], (here, peers[side]),
        )

    def beside(side, direction, owner):
        return push(
            all_planes.at[direction, owner], all_planes.at[direction, owner],
            side_send.at[side, direction], side_recv.at[side, direction], (here, peers[side]),
        )

    def onward(side, owner):
        return push(
            all_planes.at[side, owner], all_planes.at[side, owner],
            last_send.at[side], last_recv.at[side], (here, peers[side]),
        )

    def columns(turn, owner, peer):
        return push(
            wcut.at[peer], all_wcut.at[owner], w_send.at[turn - 1], w_recv.at[turn - 1], (here, peer)
        )

    sent = []

    def go(copy):
        copy.start()
        sent.append(copy)

    for direction in range(2):
        go(face(direction))
    for tensor in range(2):
        for side in range(2):
            go(ring(side, side, tensor, me))
    for direction in range(2):
        face(direction).wait_recv()
    for direction in range(2):
        for side in range(2):
            go(beside(side, side ^ direction, me))
    for turn in range(1, 4):
        go(columns(turn, me, lax.rem(me + turn, 4)))
    for tensor in range(2):
        for side in range(2):
            go(ring(side, 1 - side, tensor, me))
    for tensor in range(2):
        for side in range(2):
            ring(side, side, tensor, sources[side]).wait_recv()
            go(relay(side, tensor, sources[side]))
    for side in range(2):
        beside(side, side, sources[side]).wait_recv()
        go(onward(side, sources[side]))
    for side in range(2):
        beside(side, 1 - side, sources[side]).wait_recv()
    for turn in range(1, 4):
        origin = lax.rem(me + 4 - turn, 4)
        columns(turn, origin, origin).wait_recv()
    for side in range(2):
        for tensor in range(2):
            ring(side, 1 - side, tensor, sources[side]).wait_recv()
            relay(side, tensor, across).wait_recv()
        onward(side, across).wait_recv()
    kept.wait()
    for copy in sent:
        copy.wait_send()


def assemble_all(
    scale, table, all_feat, all_cot, all_planes, cot, bricks, prev, nxt, stage, rows, acc, part
):
    zero = jnp.zeros((8, 8, 128), jnp.float32)
    for u in range(8):
        bricks[BRICKS, u] = zero
    prev[BRICKS] = zero
    nxt[BRICKS] = zero
    def turn_brick(s, carry):
        both = jnp.concatenate(
            [all_feat[:, s].reshape(64, 512), all_cot[:, s].reshape(64, 512)], axis=0
        )
        bricks[s] = both.astype(jnp.float32).T.reshape(8, 8, 8, 128)
        return carry

    lax.fori_loop(0, BRICKS, turn_brick, 0)
    for direction, held in enumerate((prev, nxt)):
        for pair in range(BRICKS // 2):
            both = jnp.concatenate(
                [all_planes[direction, :, t, pair].reshape(64, 128) for t in range(2)], axis=0
            )
            held[2 * pair : 2 * pair + 2] = both.astype(jnp.float32).T.reshape(2, 8, 8, 128)

    acc[...] = jnp.zeros(acc.shape, jnp.float32)

    def one_brick(r, carry):
        def slot(i, j, k):
            named = table[r, 9 * i + 3 * j + k]
            return jnp.where(named < 0, BRICKS, jnp.bitwise_and(named, BRICKS - 1))

        for i in range(3):
            for j in range(3):
                vs = (slice(7, 8), slice(0, 8), slice(0, 1))[j]
                ys = (slice(0, 1), slice(1, 9), slice(9, 10))[j]
                ids = [slot(i, j, k) for k in range(3)]
                for u in range(8) if i == 1 else (0,):
                    x = (0, u + 1, 9)[i]
                    if i == 1:
                        low, mid, high = [bricks[s, u, vs] for s in ids]
                    else:
                        low, mid, high = [(prev, None, nxt)[i][s, vs] for s in ids]
                    w = lax.broadcasted_iota(jnp.int32, mid.shape, 1)
                    stage[0, x, ys] = pltpu.roll(jnp.where(w == 7, low, mid), 1, 1)
                    stage[1, x, ys] = mid
                    stage[2, x, ys] = pltpu.roll(jnp.where(w == 0, high, mid), 7, 1)
        for b in range(3):
            for c in range(3):
                j = 3 * b + c
                for x in range(10):
                    rows[r, 64 * x : 64 * x + 64, 128 * j : 128 * j + 128] = (
                        stage[c, x, b : b + 8].reshape(64, 128).astype(jnp.bfloat16)
                    )
        wide = jnp.concatenate(
            [cot[r].astype(jnp.float32), jnp.zeros((SHARE, 128), jnp.float32)], axis=1
        )
        lifted = jnp.concatenate([wide, pltpu.roll(wide, 64, 1), pltpu.roll(wide, 128, 1)], axis=0)
        acc[...] += jnp.dot(
            lifted.astype(jnp.bfloat16), rows[r], preferred_element_type=jnp.float32
        )
        return carry

    lax.fori_loop(0, BRICKS, one_brick, 0)
    lane = lax.broadcasted_iota(jnp.int32, (8, 128), 1)
    for a in range(3):
        for j in range(9):
            term = acc[16 * a : 16 * a + 16, 128 * j : 128 * j + 128] * scale
            part[9 * a + j] = jnp.where(lane < 64, term[0:8], pltpu.roll(term[8:16], 64, 1))
    for k in range(27, KERNEL_TILES):
        part[k] = jnp.zeros((8, 128), jnp.float32)


def lay_weights(weight, all_wcut, wt):
    wt[...] = jnp.zeros((128, 1152), jnp.bfloat16)
    lane = lax.broadcasted_iota(jnp.int32, (SHARE, 128), 1)
    for a in range(3):
        for j in range(9):
            k = 9 * a + j
            wt[32 * a : 32 * a + 16, 128 * j : 128 * j + 64] = weight[k]
            back = 26 - k
            block = jnp.zeros((SHARE, 128), jnp.float32)
            for p in range(4):
                start = 64 + SHARE * p
                piece = all_wcut[p, :, 128 * (back // 8) : 128 * (back // 8) + 128].astype(jnp.float32)
                piece = pltpu.roll(piece, (start - SHARE * (back % 8)) % 128, 1)
                block = jnp.where((lane >= start) & (lane < start + SHARE), piece, block)
            wt[32 * a + 16 : 32 * a + 32, 128 * j : 128 * j + 128] = block.astype(jnp.bfloat16)


def convolve(first, last, rows, wt, out, grad_in):
    def one_brick(r, carry):
        terms = lax.dot_general(
            rows[r], wt[...], (((1,), (1,)), ((), ())), preferred_element_type=jnp.float32
        )
        turned = terms.T
        total = (
            turned[0:32, 0:512]
            + pltpu.roll(turned[32:64], 640 - 64, 1)[:, 0:512]
            + turned[64:96, 128:640]
        )
        out[r] = total[0:16].astype(jnp.bfloat16)
        grad_in[r] = total[16:32].astype(jnp.bfloat16)
        return carry

    lax.fori_loop(first, last, one_brick, 0)


def conv_kernel(
    inner, outer, scale, table_at, feat_at, cot_at, planes_at, wcut_at, own_feat, own_cot, cot, weight,
    out, grad_in, result, table, all_feat, all_cot, all_planes, all_wcut, load_sem,
    bricks, prev, nxt, wt, stage, rows, acc, part, pieces, tile, blocks, whole,
    a_send, a_recv, b_send, b_recv, c_send, c_recv,
):
    here = lax.axis_index("space")
    chan = lax.axis_index("chan")
    rank = lax.rem(here, inner)
    block = here // inner
    share = KERNEL_TILES // inner

    barrier = pltpu.get_barrier_semaphore()

    def greet(d, carry):
        peer = block * inner + lax.rem(rank + d, inner)
        pl.semaphore_signal(barrier, inc=1, device_id=(peer, chan), device_id_type=MESH)
        return carry

    lax.fori_loop(1, inner, greet, 0)
    for d in range(1, outer):
        peer = lax.rem(block + d, outer) * inner + rank
        pl.semaphore_signal(barrier, inc=1, device_id=(peer, chan), device_id_type=MESH)
    loads = [
        pltpu.make_async_copy(table_at, table, load_sem.at[0]),
        pltpu.make_async_copy(planes_at, all_planes, load_sem.at[1]),
        pltpu.make_async_copy(own_feat, all_feat.at[chan], load_sem.at[2]),
        pltpu.make_async_copy(own_cot, all_cot.at[chan], load_sem.at[3]),
        pltpu.make_async_copy(wcut_at, all_wcut, load_sem.at[4]),
    ]
    for turn in range(1, 4):
        origin = lax.rem(chan + turn, 4)
        for place, (source, target) in enumerate(
            ((feat_at, all_feat), (cot_at, all_cot))
        ):
            loads.append(
                pltpu.make_async_copy(
                    source.at[origin], target.at[origin], load_sem.at[3 + 2 * turn + place]
                )
            )
    for copy in loads:
        copy.start()
    for copy in loads:
        copy.wait()
    assemble_all(
        scale, table, all_feat, all_cot, all_planes, cot, bricks, prev, nxt, stage, rows, acc, part
    )
    pl.semaphore_wait(barrier, inner - 1 + outer - 1)

    def scatter(d):
        to = lax.rem(rank + d, inner)
        return push(
            part.at[pl.ds(to * share, share)], pieces.at[d], a_send.at[d], a_recv.at[d],
            (block * inner + to, chan),
        )

    def start_scatter(d, carry):
        scatter(d).start()
        return carry

    def wait_scatter(d, carry):
        scatter(d).wait()
        return carry

    lax.fori_loop(1, inner, start_scatter, 0)
    pieces[0] = part[pl.ds(rank * share, share)]
    lay_weights(weight, all_wcut, wt)
    convolve(0, BRICKS // 2, rows, wt, out, grad_in)
    lax.fori_loop(1, inner, wait_scatter, 0)
    tile[...] = jnp.sum(pieces[...], axis=0)

    exchanges = []
    for d in range(1, outer):
        peer = lax.rem(block + d, outer)
        copy = push(
            tile, blocks.at[block], b_send.at[d - 1], b_recv.at[d - 1], (peer * inner + rank, chan)
        )
        copy.start()
        exchanges.append(copy)
    blocks[block] = tile[...]
    convolve(BRICKS // 2, BRICKS, rows, wt, out, grad_in)
    for copy in exchanges:
        copy.wait()
    mine = pl.ds(rank * share, share)
    whole[mine] = jnp.sum(blocks[...], axis=0)

    def spread(d):
        to = lax.rem(rank + d, inner)
        return push(
            whole.at[mine], whole.at[mine], c_send.at[d], c_recv.at[d], (block * inner + to, chan)
        )

    def start_spread(d, carry):
        spread(d).start()
        return carry

    def wait_spread(d, carry):
        origin = lax.rem(rank + inner - d, inner)
        theirs = pl.ds(origin * share, share)
        push(
            whole.at[theirs], whole.at[theirs], c_send.at[d], c_recv.at[d], (block * inner + origin, chan)
        ).wait_recv()
        return carry

    def sent_spread(d, carry):
        spread(d).wait_send()
        return carry

    lax.fori_loop(1, inner, start_spread, 0)
    lax.fori_loop(1, inner, wait_spread, 0)
    lax.fori_loop(1, inner, sent_spread, 0)
    for k in range(27):
        term = whole[k]
        result[k, 0:8] = term[:, 0:64]
        result[k, 8:16] = pltpu.roll(term, 64, 1)[:, 0:64]


def body(n_space, features, weight, cotangent, neighbours):
    inner = 32 if n_space % 32 == 0 else n_space // 2
    outer = n_space // inner
    vmem = pl.BlockSpec(memory_space=pltpu.VMEM)
    anyspace = pl.BlockSpec(memory_space=pl.ANY)
    bf16, f32 = jnp.bfloat16, jnp.float32

    dma = pltpu.SemaphoreType.DMA
    all_feat, all_cot, all_planes, all_wcut = pl.pallas_call(
        functools.partial(gather_kernel, n_space),
        out_shape=(
            jax.ShapeDtypeStruct((4, BRICKS, SHARE, 512), bf16),
            jax.ShapeDtypeStruct((4, BRICKS, SHARE, 512), bf16),
            jax.ShapeDtypeStruct((2, 4, 2, BRICKS // 2, SHARE, 128), bf16),
            jax.ShapeDtypeStruct((4, SHARE, 512), bf16),
        ),
        in_specs=[anyspace] * 3,
        out_specs=(anyspace,) * 4,
        scratch_shapes=[
            pltpu.VMEM((BRICKS, SHARE, 512), bf16),
            pltpu.VMEM((BRICKS, SHARE, 512), bf16),
            pltpu.VMEM((27, SHARE, 64), bf16),
            pltpu.VMEM((2, 2, BRICKS // 2, SHARE, 128), bf16),
            pltpu.VMEM((4, SHARE, 512), bf16),
            dma((4,)),
            dma((2, 2, 2)), dma((2, 2, 2)), dma((2, 2)), dma((2, 2)), dma((2,)), dma((2,)),
            dma((2, 2)), dma((2, 2)), dma((2,)), dma((2,)), dma((3,)), dma((3,)),
        ],
        compiler_params=pltpu.CompilerParams(collective_id=0, has_side_effects=True),
        name="gather",
    )(features, cotangent, weight)

    voxels = n_space * BRICKS * 512
    share = KERNEL_TILES // inner
    output, grad_input, grad_weight = pl.pallas_call(
        functools.partial(conv_kernel, inner, outer, voxels ** (-0.5)),
        out_shape=(
            jax.ShapeDtypeStruct((BRICKS, SHARE, 512), bf16),
            jax.ShapeDtypeStruct((BRICKS, SHARE, 512), bf16),
            jax.ShapeDtypeStruct((27, SHARE, 64), f32),
        ),
        in_specs=[pl.BlockSpec(memory_space=pltpu.HBM)] * 7 + [vmem] * 2,
        out_specs=(vmem,) * 3,
        scratch_shapes=[
            pltpu.SMEM((BRICKS, 27), jnp.int32),
            pltpu.VMEM((4, BRICKS, SHARE, 512), bf16),
            pltpu.VMEM((4, BRICKS, SHARE, 512), bf16),
            pltpu.VMEM((2, 4, 2, BRICKS // 2, SHARE, 128), bf16),
            pltpu.VMEM((4, SHARE, 512), bf16),
            dma((11,)),
            pltpu.VMEM((BRICKS + 1, 8, 8, 8, 128), f32),
            pltpu.VMEM((BRICKS + 1, 8, 8, 128), f32),
            pltpu.VMEM((BRICKS + 1, 8, 8, 128), f32),
            pltpu.VMEM((128, 1152), bf16),
            pltpu.VMEM((3, 10, 10, 8, 128), f32),
            pltpu.VMEM((BRICKS, 640, 1152), bf16),
            pltpu.VMEM((48, 1152), f32),
            pltpu.VMEM((KERNEL_TILES, 8, 128), f32),
            pltpu.VMEM((inner, share, 8, 128), f32),
            pltpu.VMEM((share, 8, 128), f32),
            pltpu.VMEM((outer, share, 8, 128), f32),
            pltpu.VMEM((KERNEL_TILES, 8, 128), f32),
            dma((inner,)), dma((inner,)), dma((outer - 1,)), dma((outer - 1,)),
            dma((inner,)), dma((inner,)),
        ],
        compiler_params=pltpu.CompilerParams(
            collective_id=1, has_side_effects=True, vmem_limit_bytes=63 * 2**20
        ),
        name="conv",
    )(
        neighbours, all_feat, all_cot, all_planes, all_wcut, features, cotangent, cotangent, weight
    )
    return (output, grad_input, grad_weight)


def solution(mesh):
    in_specs = (
        P("space", "chan", None),
        P(None, "chan", None),
        P("space", "chan", None),
        P("space", None),
    )
    out_specs = (P("space", "chan", None), P("space", "chan", None), P(None, "chan", None))
    return jax.shard_map(
        functools.partial(body, mesh.shape["space"]),
        mesh=mesh, in_specs=in_specs, out_specs=out_specs, check_vma=False,
    )
```

```python
import functools

import jax
import jax.numpy as jnp
from jax import lax
from jax.experimental import pallas as pl
from jax.experimental.pallas import tpu as pltpu
from jax.sharding import PartitionSpec as P

MESH = pl.DeviceIdType.MESH
BRICKS = 8
HALF = 4
SHARE = 16
KERNEL_TILES = 32


def push(source, target, send_sem, recv_sem, device):
    return pltpu.make_async_remote_copy(
        src_ref=source,
        dst_ref=target,
        send_sem=send_sem,
        recv_sem=recv_sem,
        device_id=device,
        device_id_type=MESH,
    )


def pack(feat, cot, weight, planes, wcut):
    lane = lax.broadcasted_iota(jnp.int32, (SHARE, 128), 1)
    for t, tensor in enumerate((feat, cot)):
        for pair in range(BRICKS // 2):
            for direction, lanes in enumerate((slice(384, 512), slice(0, 128))):
                first = tensor[2 * pair, :, lanes].astype(jnp.float32)
                second = tensor[2 * pair + 1, :, lanes].astype(jnp.float32)
                if direction == 0:
                    first = pltpu.roll(first, 64, 1)
                else:
                    second = pltpu.roll(second, 64, 1)
                planes[direction, t, pair] = jnp.where(lane < 64, first, second).astype(jnp.bfloat16)
    for g in range(4):
        count = min(8, 27 - 8 * g)
        block = weight[8 * g : 8 * g + count].reshape(SHARE * count, 64).astype(jnp.float32)
        if count < 8:
            block = jnp.concatenate([block, jnp.zeros((128 - SHARE * count, 64), jnp.float32)], axis=0)
        wcut[:, :, 128 * g : 128 * g + 128] = block.T.reshape(4, SHARE, 128).astype(jnp.bfloat16)


def gather_kernel(
    n_space, feat, cot, weight, all_feat, all_cot, all_planes, all_wcut,
    feat_here, cot_here, weight_here, planes, wcut, local_sem,
    ring_send, ring_recv, fwd_send, fwd_recv, face_send, face_recv,
    side_send, side_recv, last_send, last_recv, w_send, w_recv,
):
    me = lax.axis_index("chan")
    here = lax.axis_index("space")
    right, left, across = lax.rem(me + 1, 4), lax.rem(me + 3, 4), lax.rem(me + 2, 4)
    after, before = lax.rem(here + 1, n_space), lax.rem(here + n_space - 1, n_space)

    loads = [
        pltpu.make_async_copy(source, target, local_sem.at[place])
        for place, (source, target) in enumerate(
            ((feat, feat_here), (cot, cot_here), (weight, weight_here))
        )
    ]
    for copy in loads:
        copy.start()
    barrier = pltpu.get_barrier_semaphore()
    for other in (right, left, across):
        pl.semaphore_signal(barrier, inc=1, device_id=(here, other), device_id_type=MESH)
    for place in (after, before):
        pl.semaphore_signal(barrier, inc=1, device_id=(place, me), device_id_type=MESH)
    for copy in loads:
        copy.wait()
    pack(feat_here, cot_here, weight_here, planes, wcut)
    kept = pltpu.make_async_copy(wcut.at[me], all_wcut.at[me], local_sem.at[3])
    kept.start()
    pl.semaphore_wait(barrier, 5)

    peers = (right, left)
    sources = (left, right)
    pairs = ((feat, all_feat), (cot, all_cot))

    def face(direction):
        return push(
            planes.at[direction], all_planes.at[direction, me],
            face_send.at[direction], face_recv.at[direction], ((after, before)[direction], me),
        )

    def ring(side, half, tensor, owner):
        own, every = pairs[tensor]
        rows = pl.ds(HALF * half, HALF)
        return push(
            own.at[rows], every.at[owner, rows],
            ring_send.at[side, half, tensor], ring_recv.at[side, half, tensor], (here, peers[side]),
        )

    def relay(side, tensor, owner):
        every = pairs[tensor][1]
        rows = pl.ds(HALF * side, HALF)
        return push(
            every.at[owner, rows], every.at[owner, rows],
            fwd_send.at[side, tensor], fwd_recv.at[side, tensor], (here, peers[side]),
        )

    def beside(side, direction, owner):
        return push(
            all_planes.at[direction, owner], all_planes.at[direction, owner],
            side_send.at[side, direction], side_recv.at[side, direction], (here, peers[side]),
        )

    def onward(side, owner):
        return push(
            all_planes.at[side, owner], all_planes.at[side, owner],
            last_send.at[side], last_recv.at[side], (here, peers[side]),
        )

    def columns(turn, owner, peer):
        return push(
            wcut.at[peer], all_wcut.at[owner], w_send.at[turn - 1], w_recv.at[turn - 1], (here, peer)
        )

    sent = []

    def go(copy):
        copy.start()
        sent.append(copy)

    for direction in range(2):
        go(face(direction))
    for tensor in range(2):
        for side in range(2):
            go(ring(side, side, tensor, me))
    for direction in range(2):
        face(direction).wait_recv()
    for direction in range(2):
        for side in range(2):
            go(beside(side, side ^ direction, me))
    for turn in range(1, 4):
        go(columns(turn, me, lax.rem(me + turn, 4)))
    for tensor in range(2):
        for side in range(2):
            go(ring(side, 1 - side, tensor, me))
    for tensor in range(2):
        for side in range(2):
            ring(side, side, tensor, sources[side]).wait_recv()
            go(relay(side, tensor, sources[side]))
    for side in range(2):
        beside(side, side, sources[side]).wait_recv()
        go(onward(side, sources[side]))
    for side in range(2):
        beside(side, 1 - side, sources[side]).wait_recv()
    for turn in range(1, 4):
        origin = lax.rem(me + 4 - turn, 4)
        columns(turn, origin, origin).wait_recv()
    for side in range(2):
        for tensor in range(2):
            ring(side, 1 - side, tensor, sources[side]).wait_recv()
            relay(side, tensor, across).wait_recv()
        onward(side, across).wait_recv()
    kept.wait()
    for copy in sent:
        copy.wait_send()


def assemble_all(
    scale, table, all_feat, all_cot, all_planes, cot, bricks, prev, nxt, stage, rows, acc, part
):
    zero = jnp.zeros((8, 8, 128), jnp.float32)
    for u in range(8):
        bricks[BRICKS, u] = zero
    prev[BRICKS] = zero
    nxt[BRICKS] = zero
    def turn_brick(s, carry):
        both = jnp.concatenate(
            [all_feat[:, s].reshape(64, 512), all_cot[:, s].reshape(64, 512)], axis=0
        )
        bricks[s] = both.astype(jnp.float32).T.reshape(8, 8, 8, 128)
        return carry

    lax.fori_loop(0, BRICKS, turn_brick, 0, unroll=True)
    for direction, held in enumerate((prev, nxt)):
        for pair in range(BRICKS // 2):
            both = jnp.concatenate(
                [all_planes[direction, :, t, pair].reshape(64, 128) for t in range(2)], axis=0
            )
            held[2 * pair : 2 * pair + 2] = both.astype(jnp.float32).T.reshape(2, 8, 8, 128)

    acc[...] = jnp.zeros(acc.shape, jnp.float32)

    def one_brick(r, side):
        def slot(i, j, k):
            named = table[r, 9 * i + 3 * j + k]
            return jnp.where(named < 0, BRICKS, jnp.bitwise_and(named, BRICKS - 1))

        for i in range(3):
            for j in range(3):
                vs = (slice(7, 8), slice(0, 8), slice(0, 1))[j]
                ys = (slice(0, 1), slice(1, 9), slice(9, 10))[j]
                ids = [slot(i, j, k) for k in range(3)]
                for u in range(8) if i == 1 else (0,):
                    x = (0, u + 1, 9)[i]
                    if i == 1:
                        low, mid, high = [bricks[s, u, vs] for s in ids]
                    else:
                        low, mid, high = [(prev, None, nxt)[i][s, vs] for s in ids]
                    w = lax.broadcasted_iota(jnp.int32, mid.shape, 1)
                    stage[side, 0, x, ys] = pltpu.roll(jnp.where(w == 7, low, mid), 1, 1)
                    stage[side, 1, x, ys] = mid
                    stage[side, 2, x, ys] = pltpu.roll(jnp.where(w == 0, high, mid), 7, 1)
        for b in range(3):
            for c in range(3):
                j = 3 * b + c
                for x in range(10):
                    rows[r, 64 * x : 64 * x + 64, 128 * j : 128 * j + 128] = (
                        stage[side, c, x, b : b + 8].reshape(64, 128).astype(jnp.bfloat16)
                    )
        wide = jnp.concatenate(
            [cot[r].astype(jnp.float32), jnp.zeros((SHARE, 128), jnp.float32)], axis=1
        )
        lifted = jnp.concatenate([wide, pltpu.roll(wide, 64, 1), pltpu.roll(wide, 128, 1)], axis=0)
        acc[...] += jnp.dot(
            lifted.astype(jnp.bfloat16), rows[r], preferred_element_type=jnp.float32
        )

    def two_bricks(t, carry):
        one_brick(2 * t, 0)
        one_brick(2 * t + 1, 1)
        return carry

    lax.fori_loop(0, BRICKS // 2, two_bricks, 0)
    lane = lax.broadcasted_iota(jnp.int32, (8, 128), 1)
    for a in range(3):
        for j in range(9):
            term = acc[16 * a : 16 * a + 16, 128 * j : 128 * j + 128] * scale
            part[9 * a + j] = jnp.where(lane < 64, term[0:8], pltpu.roll(term[8:16], 64, 1))
    for k in range(27, KERNEL_TILES):
        part[k] = jnp.zeros((8, 128), jnp.float32)


def lay_weights(weight, all_wcut, wt):
    wt[...] = jnp.zeros((128, 1152), jnp.bfloat16)
    lane = lax.broadcasted_iota(jnp.int32, (SHARE, 128), 1)
    for a in range(3):
        for j in range(9):
            k = 9 * a + j
            wt[32 * a : 32 * a + 16, 128 * j : 128 * j + 64] = weight[k]
            back = 26 - k
            block = jnp.zeros((SHARE, 128), jnp.float32)
            for p in range(4):
                start = 64 + SHARE * p
                piece = all_wcut[p, :, 128 * (back // 8) : 128 * (back // 8) + 128].astype(jnp.float32)
                piece = pltpu.roll(piece, (start - SHARE * (back % 8)) % 128, 1)
                block = jnp.where((lane >= start) & (lane < start + SHARE), piece, block)
            wt[32 * a + 16 : 32 * a + 32, 128 * j : 128 * j + 128] = block.astype(jnp.bfloat16)


def convolve(first, last, rows, wt, out, grad_in):
    def one_brick(r, carry):
        terms = lax.dot_general(
            rows[r], wt[...], (((1,), (1,)), ((), ())), preferred_element_type=jnp.float32
        )
        turned = terms.T
        total = (
            turned[0:32, 0:512]
            + pltpu.roll(turned[32:64], 640 - 64, 1)[:, 0:512]
            + turned[64:96, 128:640]
        )
        out[r] = total[0:16].astype(jnp.bfloat16)
        grad_in[r] = total[16:32].astype(jnp.bfloat16)
        return carry

    lax.fori_loop(first, last, one_brick, 0, unroll=True)


def conv_kernel(
    inner, outer, scale, table_at, feat_at, cot_at, planes_at, wcut_at, own_feat, own_cot, cot, weight,
    out, grad_in, result, table, all_feat, all_cot, all_planes, all_wcut, load_sem,
    bricks, prev, nxt, wt, stage, rows, acc, part, pieces, tile, blocks, whole,
    a_send, a_recv, b_send, b_recv, c_send, c_recv,
):
    here = lax.axis_index("space")
    chan = lax.axis_index("chan")
    rank = lax.rem(here, inner)
    block = here // inner
    share = KERNEL_TILES // inner

    barrier = pltpu.get_barrier_semaphore()

    def greet(d, carry):
        peer = block * inner + lax.rem(rank + d, inner)
        pl.semaphore_signal(barrier, inc=1, device_id=(peer, chan), device_id_type=MESH)
        return carry

    lax.fori_loop(1, inner, greet, 0)
    for d in range(1, outer):
        peer = lax.rem(block + d, outer) * inner + rank
        pl.semaphore_signal(barrier, inc=1, device_id=(peer, chan), device_id_type=MESH)
    loads = [
        pltpu.make_async_copy(table_at, table, load_sem.at[0]),
        pltpu.make_async_copy(planes_at, all_planes, load_sem.at[1]),
        pltpu.make_async_copy(own_feat, all_feat.at[chan], load_sem.at[2]),
        pltpu.make_async_copy(own_cot, all_cot.at[chan], load_sem.at[3]),
        pltpu.make_async_copy(wcut_at, all_wcut, load_sem.at[4]),
    ]
    for turn in range(1, 4):
        origin = lax.rem(chan + turn, 4)
        for place, (source, target) in enumerate(
            ((feat_at, all_feat), (cot_at, all_cot))
        ):
            loads.append(
                pltpu.make_async_copy(
                    source.at[origin], target.at[origin], load_sem.at[3 + 2 * turn + place]
                )
            )
    for copy in loads:
        copy.start()
    for copy in loads:
        copy.wait()
    assemble_all(
        scale, table, all_feat, all_cot, all_planes, cot, bricks, prev, nxt, stage, rows, acc, part
    )
    pl.semaphore_wait(barrier, inner - 1 + outer - 1)

    def scatter(d):
        to = lax.rem(rank + d, inner)
        return push(
            part.at[pl.ds(to * share, share)], pieces.at[d], a_send.at[d], a_recv.at[d],
            (block * inner + to, chan),
        )

    def start_scatter(d, carry):
        scatter(d).start()
        return carry

    def wait_scatter(d, carry):
        scatter(d).wait()
        return carry

    lax.fori_loop(1, inner, start_scatter, 0)
    pieces[0] = part[pl.ds(rank * share, share)]
    lay_weights(weight, all_wcut, wt)
    convolve(0, BRICKS // 2, rows, wt, out, grad_in)
    lax.fori_loop(1, inner, wait_scatter, 0)
    tile[...] = jnp.sum(pieces[...], axis=0)

    exchanges = []
    for d in range(1, outer):
        peer = lax.rem(block + d, outer)
        copy = push(
            tile, blocks.at[block], b_send.at[d - 1], b_recv.at[d - 1], (peer * inner + rank, chan)
        )
        copy.start()
        exchanges.append(copy)
    blocks[block] = tile[...]
    convolve(BRICKS // 2, BRICKS, rows, wt, out, grad_in)
    for copy in exchanges:
        copy.wait()
    mine = pl.ds(rank * share, share)
    whole[mine] = jnp.sum(blocks[...], axis=0)

    def spread(d):
        to = lax.rem(rank + d, inner)
        return push(
            whole.at[mine], whole.at[mine], c_send.at[d], c_recv.at[d], (block * inner + to, chan)
        )

    def start_spread(d, carry):
        spread(d).start()
        return carry

    def wait_spread(d, carry):
        origin = lax.rem(rank + inner - d, inner)
        theirs = pl.ds(origin * share, share)
        push(
            whole.at[theirs], whole.at[theirs], c_send.at[d], c_recv.at[d], (block * inner + origin, chan)
        ).wait_recv()
        return carry

    def sent_spread(d, carry):
        spread(d).wait_send()
        return carry

    lax.fori_loop(1, inner, start_spread, 0)
    lax.fori_loop(1, inner, wait_spread, 0)
    lax.fori_loop(1, inner, sent_spread, 0)
    for k in range(27):
        term = whole[k]
        result[k, 0:8] = term[:, 0:64]
        result[k, 8:16] = pltpu.roll(term, 64, 1)[:, 0:64]


def body(n_space, features, weight, cotangent, neighbours):
    inner = 32 if n_space % 32 == 0 else n_space // 2
    outer = n_space // inner
    vmem = pl.BlockSpec(memory_space=pltpu.VMEM)
    anyspace = pl.BlockSpec(memory_space=pl.ANY)
    bf16, f32 = jnp.bfloat16, jnp.float32

    dma = pltpu.SemaphoreType.DMA
    all_feat, all_cot, all_planes, all_wcut = pl.pallas_call(
        functools.partial(gather_kernel, n_space),
        out_shape=(
            jax.ShapeDtypeStruct((4, BRICKS, SHARE, 512), bf16),
            jax.ShapeDtypeStruct((4, BRICKS, SHARE, 512), bf16),
            jax.ShapeDtypeStruct((2, 4, 2, BRICKS // 2, SHARE, 128), bf16),
            jax.ShapeDtypeStruct((4, SHARE, 512), bf16),
        ),
        in_specs=[anyspace] * 3,
        out_specs=(anyspace,) * 4,
        scratch_shapes=[
            pltpu.VMEM((BRICKS, SHARE, 512), bf16),
            pltpu.VMEM((BRICKS, SHARE, 512), bf16),
            pltpu.VMEM((27, SHARE, 64), bf16),
            pltpu.VMEM((2, 2, BRICKS // 2, SHARE, 128), bf16),
            pltpu.VMEM((4, SHARE, 512), bf16),
            dma((4,)),
            dma((2, 2, 2)), dma((2, 2, 2)), dma((2, 2)), dma((2, 2)), dma((2,)), dma((2,)),
            dma((2, 2)), dma((2, 2)), dma((2,)), dma((2,)), dma((3,)), dma((3,)),
        ],
        compiler_params=pltpu.CompilerParams(collective_id=0, has_side_effects=True),
        name="gather",
    )(features, cotangent, weight)

    voxels = n_space * BRICKS * 512
    share = KERNEL_TILES // inner
    output, grad_input, grad_weight = pl.pallas_call(
        functools.partial(conv_kernel, inner, outer, voxels ** (-0.5)),
        out_shape=(
            jax.ShapeDtypeStruct((BRICKS, SHARE, 512), bf16),
            jax.ShapeDtypeStruct((BRICKS, SHARE, 512), bf16),
            jax.ShapeDtypeStruct((27, SHARE, 64), f32),
        ),
        in_specs=[pl.BlockSpec(memory_space=pltpu.HBM)] * 7 + [vmem] * 2,
        out_specs=(vmem,) * 3,
        scratch_shapes=[
            pltpu.SMEM((BRICKS, 27), jnp.int32),
            pltpu.VMEM((4, BRICKS, SHARE, 512), bf16),
            pltpu.VMEM((4, BRICKS, SHARE, 512), bf16),
            pltpu.VMEM((2, 4, 2, BRICKS // 2, SHARE, 128), bf16),
            pltpu.VMEM((4, SHARE, 512), bf16),
            dma((11,)),
            pltpu.VMEM((BRICKS + 1, 8, 8, 8, 128), f32),
            pltpu.VMEM((BRICKS + 1, 8, 8, 128), f32),
            pltpu.VMEM((BRICKS + 1, 8, 8, 128), f32),
            pltpu.VMEM((128, 1152), bf16),
            pltpu.VMEM((2, 3, 10, 10, 8, 128), f32),
            pltpu.VMEM((BRICKS, 640, 1152), bf16),
            pltpu.VMEM((48, 1152), f32),
            pltpu.VMEM((KERNEL_TILES, 8, 128), f32),
            pltpu.VMEM((inner, share, 8, 128), f32),
            pltpu.VMEM((share, 8, 128), f32),
            pltpu.VMEM((outer, share, 8, 128), f32),
            pltpu.VMEM((KERNEL_TILES, 8, 128), f32),
            dma((inner,)), dma((inner,)), dma((outer - 1,)), dma((outer - 1,)),
            dma((inner,)), dma((inner,)),
        ],
        compiler_params=pltpu.CompilerParams(
            collective_id=1, has_side_effects=True, vmem_limit_bytes=63 * 2**20
        ),
        name="conv",
    )(
        neighbours, all_feat, all_cot, all_planes, all_wcut, features, cotangent, cotangent, weight
    )
    return (output, grad_input, grad_weight)


def solution(mesh):
    in_specs = (
        P("space", "chan", None),
        P(None, "chan", None),
        P("space", "chan", None),
        P("space", None),
    )
    out_specs = (P("space", "chan", None), P("space", "chan", None), P(None, "chan", None))
    return jax.shard_map(
        functools.partial(body, mesh.shape["space"]),
        mesh=mesh, in_specs=in_specs, out_specs=out_specs, check_vma=False,
    )
```
